32 devices in a mesh: dp: 4 (over z), row: 4 (over y, x), col: 2 (over core).
Axes of the slice: x: 2, y: 2, z: 4, core: 2. Of those that a mesh axis runs over, the one named last changes fastest.
Arguments:
- layer_in: bfloat16 [1024, 2048], P('dp', ('row', 'col')), as said below
- doc_ids: int32 [1024], P('dp'), may hold values from 0 to 255, as said below
- positions: int32 [1024], P('dp'), may hold values from 0 to 510, as said below
- attn_gain: float32 [2048], P(('row', 'col')), may hold values from 0.1 to 1.9
- query_weight: bfloat16 [2048, 2048], P('row', 'col'), as said below
- key_weight: bfloat16 [2048, 512], P('row', 'col'), as said below
- value_weight: bfloat16 [2048, 512], P('row', 'col'), may hold values from -0.125 to 0.125
- out_weight: bfloat16 [2048, 2048], P('col', 'row'), may hold values from -0.5 to 0.5
- mlp_gain: float32 [2048], P(('row', 'col')), may hold values from 0.1 to 1.9
- gate_weight: bfloat16 [2048, 8192], P('row', 'col'), may hold values from -0.125 to 0.125
- up_weight: bfloat16 [2048, 8192], P('row', 'col'), may hold values from -0.125 to 0.125
- down_weight: bfloat16 [8192, 2048], P('col', 'row'), may hold values from -0.0625 to 0.0625
- cotangent: bfloat16 [1024, 2048], P('dp', ('row', 'col')), may hold values from -6 to 6
Outputs:
- layer_out: bfloat16 [1024, 2048], P('dp', ('row', 'col'))
- input_grad: float32 [1024, 2048], P('dp', ('row', 'col'))
- attn_gain_grad: float32 [2048], P(('row', 'col'))
- query_grad: float32 [2048, 2048], P('row', 'col')
- key_grad: float32 [2048, 512], P('row', 'col')
- value_grad: float32 [2048, 512], P('row', 'col')
- outproj_grad: float32 [2048, 2048], P('col', 'row')
- mlp_gain_grad: float32 [2048], P(('row', 'col'))
- gate_grad: float32 [2048, 8192], P('row', 'col')
- up_grad: float32 [2048, 8192], P('row', 'col')
- down_grad: float32 [8192, 2048], P('col', 'row')
The draws below stay inside these ranges and needn't reach their ends.
Inputs may be any that keep to these rules, and one draw needn't show every extreme that they name: `doc_ids`: A token's id is the row, within its index of dp, of the first token of its sequence; within one index of dp the ids never fall; a sequence lies wholly in that index's 256 rows and has 1 to 256 tokens; some sequence has exactly 256 tokens. Along a sequence the positions rise by one from a start of the sequence's own, below 256. `layer_in`: Real-valued, entries up to about 30 in magnitude, with scales that vary by feature. `query_weight`: weights of order fan-in to the minus one half. `key_weight`: weights of order fan-in to the minus one half.
All inputs are finite; a program needn't handle non-finite values.
Results may differ from the reference program's by a relative error of at most 0.013.
Values may be sent and summed in bfloat16 or wider, within the bound.
No kernel may reach another device: no remote copies, remote signals or barrier semaphores. Data moves between devices by JAX's collectives and lax.ppermute only.
A program may use at most 192 MiB of HBM per device.

```python
import math
import jax
import jax.numpy as jnp
from jax import lax

D = 2048
QH = 32
KVH = 8
HD = 64
FF = 8192
TOK_DEV = 256
QD = 2048
KD = 512
SEQ_MAX = 256
TOKENS = 1024


def doc_layout(key):
    groups = TOKENS // TOK_DEV
    base_key = jax.random.fold_in(key, 7)
    count_key, cut_key, whole_key, shift_key = jax.random.split(base_key, 4)
    index = jnp.arange(TOK_DEV, dtype=jnp.int32)
    group_index = jnp.arange(groups, dtype=jnp.int32)
    extra = jax.random.randint(count_key, (groups,), 0, 8)
    chosen = jax.random.randint(whole_key, (), 0, groups).astype(jnp.int32)
    forced = (chosen + 1) % groups
    extra = jnp.where(group_index == chosen, 0, extra)
    cuts = jax.random.randint(cut_key, (groups, 7), 1, TOK_DEV)
    used = jnp.arange(7)[None, :] < extra[:, None]
    hits = (cuts[:, :, None] == index[None, None, :]) & used[:, :, None]
    last_start = (group_index == forced)[:, None] & (index == TOK_DEV - 1)[None, :]
    starts = jnp.any(hits, axis=1) | (index % SEQ_MAX == 0)[None, :] | last_start
    docs = (jnp.cumsum(starts.astype(jnp.int32), axis=1) - 1).astype(jnp.int32)
    first = lax.cummax(jnp.where(starts, index[None, :], 0), axis=1).astype(jnp.int32)
    shifts = jax.random.randint(shift_key, (groups, TOK_DEV), 0, SEQ_MAX)
    shift_doc = jnp.take_along_axis(shifts, docs, axis=1)
    shift_doc = jnp.where((group_index == chosen)[:, None] & (docs == 0), SEQ_MAX - 1, shift_doc)
    shift_doc = jnp.where(last_start, 0, shift_doc)
    places = (index[None, :] - first + shift_doc).astype(jnp.int32)
    return (first, places)


def draw_doc_ids(key, part):
    return doc_layout(key)[0].reshape(TOKENS).astype(jnp.int32)


def draw_positions(key, part):
    return doc_layout(key)[1].reshape(TOKENS).astype(jnp.int32)


def draw_layer_in(key, part):
    index = jnp.arange(D, dtype=jnp.float32)
    rising = jnp.exp(jnp.log(3.0) * index / D)
    return (jax.random.normal(key, (TOKENS, D), jnp.float32) * rising[None, :]).astype(jnp.bfloat16)


def query_key(key):
    first_key, second_key = jax.random.split(jax.random.fold_in(key, 3))
    query_part = jax.random.normal(first_key, (D, QD), jnp.float32) * D ** (-0.5)
    key_part = jax.random.normal(second_key, (D, KD), jnp.float32) * D ** (-0.5)
    return (query_part, key_part)


def draw_query_weight(key, part):
    return query_key(key)[0].astype(jnp.bfloat16)


def draw_key_weight(key, part):
    return query_key(key)[1].astype(jnp.bfloat16)


def block_levels(stream_key, dims, pieces, low, high):
    level, own = 1.0, jax.random.fold_in(stream_key, 6)
    for dim, shards_of in pieces:
        draws = jnp.exp(jax.random.uniform(jax.random.fold_in(own, dim), (shards_of,), jnp.float32, low / len(pieces), high / len(pieces)))
        level = level * jnp.repeat(draws, dims[dim] // shards_of).reshape([-1 if axis == dim else 1 for axis in range(len(dims))])
    return level


def noise(key, shape, scale, reach, shards=(), kind=jnp.bfloat16):
    entries = jax.random.normal(key, shape, jnp.float32) * scale
    if len(shards) > 0:
        entries = block_levels(key, shape, shards, -0.22, 0.18) * entries
    return jnp.clip(entries, min=-reach, max=reach).astype(kind)


def setup_inputs(seed: int = 0) -> dict:
    splits = jax.random.split(jax.random.key(seed), 14)
    layer_in = draw_layer_in(jax.random.fold_in(splits[13], 71), 0)
    doc_ids = draw_doc_ids(jax.random.fold_in(splits[13], 71), 0)
    positions = draw_positions(jax.random.fold_in(splits[13], 71), 0)
    attn_gain = jnp.clip(1.0 + 0.18 * jax.random.normal(splits[3], (D,), jnp.float32), 0.1, 1.9)
    query_weight = draw_query_weight(jax.random.fold_in(splits[13], 71), 0)
    key_weight = draw_key_weight(jax.random.fold_in(splits[13], 71), 0)
    value_weight = noise(splits[6], (D, KD), D ** -0.5, 0.125, ((0, 4), (1, 2)))
    out_weight = noise(splits[7], (QD, D), (QD // 16) ** -0.5, 0.5, ((0, 2), (1, 4)))
    mlp_gain = jnp.clip(1.0 + 0.18 * jax.random.normal(splits[8], (D,), jnp.float32), 0.1, 1.9)
    gate_weight = noise(splits[9], (D, FF), D ** -0.5, 0.125, ((0, 4), (1, 2)))
    up_weight = noise(splits[10], (D, FF), D ** -0.5, 0.125, ((0, 4), (1, 2)))
    down_weight = noise(splits[11], (FF, D), FF ** -0.5, 0.0625, ((0, 2), (1, 4)))
    cotangent = noise(splits[12], (TOKENS, D), 1.0, 6.0, ((0, 4), (1, 8)))
    return dict(layer_in=layer_in, doc_ids=doc_ids, positions=positions, attn_gain=attn_gain, query_weight=query_weight, key_weight=key_weight, value_weight=value_weight, out_weight=out_weight, mlp_gain=mlp_gain, gate_weight=gate_weight, up_weight=up_weight, down_weight=down_weight, cotangent=cotangent)


EPSILON = 1e-05
LOG_BASE = math.log(500000.0)
NEG_FILL = -1e+30

def rope_tables(positions, width):
    half_width = width // 2
    frequency = jnp.exp(-(2.0 * jnp.arange(half_width, dtype=jnp.float32) / width) * LOG_BASE)
    angles = positions.astype(jnp.float32)[:, None] * frequency[None, :]
    return (jnp.cos(angles), jnp.sin(angles))

def rotate(values, cosine, sine):
    half_width = values.shape[-1] // 2
    front = values[..., :half_width]
    back = values[..., half_width:]
    return jnp.concatenate([front * cosine - back * sine, back * cosine + front * sine], axis=-1)

def layer_group(stream_in, doc_group, pos_group, cot_group, attn_gain, query_weight, key_weight, value_weight, out_weight, mlp_gain, gate_weight, up_weight, down_weight):
    count_rows = stream_in.shape[0]
    group_size = QH // KVH
    score_scale = HD ** (-0.5)
    stream = stream_in.astype(jnp.float32)
    inv_one = lax.rsqrt(lax.optimization_barrier(jnp.mean(stream * stream, axis=1, keepdims=True)) + EPSILON)
    normed_one = stream * inv_one
    attn_input = (normed_one * attn_gain).astype(jnp.bfloat16)
    query_lin = jnp.dot(attn_input, query_weight, preferred_element_type=jnp.float32)
    key_lin = jnp.dot(attn_input, key_weight, preferred_element_type=jnp.float32)
    value_lin = jnp.dot(attn_input, value_weight, preferred_element_type=jnp.float32)
    values = value_lin.astype(jnp.bfloat16).reshape(count_rows, KVH, HD)
    cosine, sine = rope_tables(pos_group, HD)
    queries = rotate(query_lin.reshape(count_rows, QH, HD), cosine[:, None, :], sine[:, None, :]).astype(jnp.bfloat16)
    keys = rotate(key_lin.reshape(count_rows, KVH, HD), cosine[:, None, :], sine[:, None, :]).astype(jnp.bfloat16)
    query_wide = queries.reshape(count_rows, KVH, group_size, HD).astype(jnp.float32)
    key_wide = keys.astype(jnp.float32)
    value_wide = values.astype(jnp.float32)
    row_ids = jnp.arange(count_rows)
    allowed = (doc_group[:, None] == doc_group[None, :]) & (row_ids[:, None] >= row_ids[None, :])
    scores = jnp.einsum('qkgd,skd->kgqs', query_wide, key_wide) * score_scale
    scores = jnp.where(allowed[None, None], scores, NEG_FILL)
    top_score = lax.optimization_barrier(jnp.max(scores, axis=-1, keepdims=True))
    log_total = top_score + jnp.log(lax.optimization_barrier(jnp.sum(jnp.exp(scores - top_score), axis=-1, keepdims=True)))
    probs = jnp.exp(scores - log_total)
    probs_low = probs.astype(jnp.bfloat16)
    attn_heads = jnp.einsum('kgqs,skd->qkgd', probs_low.astype(jnp.float32), value_wide).reshape(count_rows, QD).astype(jnp.bfloat16)
    mid = stream + jnp.dot(attn_heads, out_weight, preferred_element_type=jnp.float32)
    inv_two = lax.rsqrt(lax.optimization_barrier(jnp.mean(mid * mid, axis=1, keepdims=True)) + EPSILON)
    normed_two = mid * inv_two
    mlp_input = (normed_two * mlp_gain).astype(jnp.bfloat16)
    gate = jnp.dot(mlp_input, gate_weight, preferred_element_type=jnp.float32)
    up_lin = jnp.dot(mlp_input, up_weight, preferred_element_type=jnp.float32)
    sigmoid = jax.nn.sigmoid(gate)
    hidden = (gate * sigmoid * up_lin).astype(jnp.bfloat16)
    layer_out = (mid + jnp.dot(hidden, down_weight, preferred_element_type=jnp.float32)).astype(jnp.bfloat16)
    d_hidden = jnp.dot(cot_group, down_weight.T, preferred_element_type=jnp.float32)
    d_gate = (d_hidden * up_lin * (sigmoid * (1.0 + gate * (1.0 - sigmoid)))).astype(jnp.bfloat16)
    d_up = (d_hidden * gate * sigmoid).astype(jnp.bfloat16)
    down_grad = jnp.dot(hidden.T, cot_group, preferred_element_type=jnp.float32)
    gate_grad = jnp.dot(mlp_input.T, d_gate, preferred_element_type=jnp.float32)
    up_grad = jnp.dot(mlp_input.T, d_up, preferred_element_type=jnp.float32)
    d_norm_two = jnp.dot(d_gate, gate_weight.T, preferred_element_type=jnp.float32) + jnp.dot(d_up, up_weight.T, preferred_element_type=jnp.float32)
    mlp_gain_grad = lax.optimization_barrier(jnp.sum(d_norm_two * mid * inv_two, axis=0))
    g_two = d_norm_two * mlp_gain
    d_mid = cot_group.astype(jnp.float32) + inv_two * (g_two - normed_two * lax.optimization_barrier(jnp.mean(g_two * normed_two, axis=1, keepdims=True)))
    d_mid_low = d_mid.astype(jnp.bfloat16)
    outproj_grad = jnp.dot(attn_heads.T, d_mid_low, preferred_element_type=jnp.float32)
    d_heads = jnp.dot(d_mid_low, out_weight.T, preferred_element_type=jnp.float32).astype(jnp.bfloat16)
    d_heads_wide = d_heads.reshape(count_rows, KVH, group_size, HD).astype(jnp.float32)
    attn_wide = attn_heads.reshape(count_rows, KVH, group_size, HD).astype(jnp.float32)
    d_values = jnp.einsum('kgqs,qkgd->skd', probs_low.astype(jnp.float32), d_heads_wide).astype(jnp.bfloat16)
    d_probs = jnp.einsum('qkgd,skd->kgqs', d_heads_wide, value_wide)
    delta = jnp.einsum('qkgd,qkgd->kgq', d_heads_wide, attn_wide)
    d_scores = (probs * (d_probs - delta[..., None]) * score_scale).astype(jnp.bfloat16)
    d_scores_wide = d_scores.astype(jnp.float32)
    d_rot_q = jnp.einsum('kgqs,skd->qkgd', d_scores_wide, key_wide).reshape(count_rows, QH, HD)
    d_rot_k = jnp.einsum('kgqs,qkgd->skd', d_scores_wide, query_wide)
    d_query = rotate(d_rot_q, cosine[:, None, :], -sine[:, None, :]).reshape(count_rows, QD).astype(jnp.bfloat16)
    d_key = rotate(d_rot_k, cosine[:, None, :], -sine[:, None, :]).reshape(count_rows, KD).astype(jnp.bfloat16)
    d_value_rows = d_values.reshape(count_rows, KD)
    query_grad = jnp.dot(attn_input.T, d_query, preferred_element_type=jnp.float32)
    key_grad = jnp.dot(attn_input.T, d_key, preferred_element_type=jnp.float32)
    value_grad = jnp.dot(attn_input.T, d_value_rows, preferred_element_type=jnp.float32)
    d_norm_one = jnp.dot(d_query, query_weight.T, preferred_element_type=jnp.float32) + jnp.dot(d_key, key_weight.T, preferred_element_type=jnp.float32) + jnp.dot(d_value_rows, value_weight.T, preferred_element_type=jnp.float32)
    attn_gain_grad = lax.optimization_barrier(jnp.sum(d_norm_one * stream * inv_one, axis=0))
    g_one = d_norm_one * attn_gain
    input_grad = d_mid + inv_one * (g_one - normed_one * lax.optimization_barrier(jnp.mean(g_one * normed_one, axis=1, keepdims=True)))
    grads = (attn_gain_grad, query_grad, key_grad, value_grad, outproj_grad, mlp_gain_grad, gate_grad, up_grad, down_grad)
    return (layer_out, input_grad, grads)

def reference(layer_in, doc_ids, positions, attn_gain, query_weight, key_weight, value_weight, out_weight, mlp_gain, gate_weight, up_weight, down_weight, cotangent):
    groups = TOKENS // TOK_DEV

    def by_group(array):
        return array.reshape((groups, TOK_DEV) + array.shape[1:])
    shapes = [(D,), (D, QD), (D, KD), (D, KD), (QD, D), (D,), (D, FF), (D, FF), (FF, D)]
    starting = tuple((jnp.zeros(shape_one, jnp.float32) for shape_one in shapes))

    def accumulate(totals, batch_items):
        stream_in, doc_group, pos_group, cot_group = batch_items
        layer_out, input_grad, grads = layer_group(stream_in, doc_group, pos_group, cot_group, attn_gain, query_weight, key_weight, value_weight, out_weight, mlp_gain, gate_weight, up_weight, down_weight)
        return (tuple((total + grad_one for total, grad_one in zip(totals, grads))), (layer_out, input_grad))
    totals, (outs_group, grads_group) = lax.scan(accumulate, starting, (by_group(layer_in), by_group(doc_ids), by_group(positions), by_group(cotangent)))
    layer_out = outs_group.reshape(TOKENS, D)
    input_grad = grads_group.reshape(TOKENS, D)
    return (layer_out, input_grad, totals[0], totals[1], totals[2], totals[3], totals[4], totals[5], totals[6], totals[7], totals[8])
```

```python
import functools
import math

import jax
import jax.numpy as jnp
from jax import lax
from jax.experimental import pallas as pl
from jax.experimental.pallas import tpu as pltpu
from jax.sharding import PartitionSpec as P

HD = 64
HALF = HD // 2
EPSILON = 1e-05
LOG_BASE = math.log(500000.0)
NEG_FILL = -1e30
PAD = 16
F32 = jnp.float32
BF16 = jnp.bfloat16


NN = (((1,), (0,)), ((), ()))
NT = (((1,), (1,)), ((), ()))
TN = (((0,), (0,)), ((), ()))


def mm(a, b, dims=NN):
    return lax.dot_general(a, b, dims, preferred_element_type=F32)


def iota(shape, dim):
    return lax.broadcasted_iota(jnp.int32, shape, dim)


def eye_mask(n):
    return iota((n, n), 0) == iota((n, n), 1)


def col_to_row(col):
    n = col.shape[0]
    wide = jnp.broadcast_to(col, (n, n))
    return jnp.sum(jnp.where(eye_mask(n), wide, 0.0), axis=0, keepdims=True)


def row_to_col(row):
    n = row.shape[1]
    wide = jnp.broadcast_to(row, (n, n))
    return jnp.sum(jnp.where(eye_mask(n), wide, 0.0), axis=1, keepdims=True)


def pack_row(row):
    n = row.shape[1]
    high = row.astype(BF16).astype(F32)
    rest = row - high
    middle = rest.astype(BF16).astype(F32)
    low = rest - middle
    sub = iota((PAD, n), 0)
    out = jnp.where(sub == 0, high, jnp.where(sub == 1, middle, jnp.where(sub == 2, low, 0.0)))
    return out.astype(BF16)


def unpack_row(block):
    return jnp.sum(block.astype(F32), axis=0, keepdims=True)


def rope_apply(values, cosine, sine):
    lanes = iota(values.shape, 1)
    front = (lanes % HD) < HALF
    width = values.shape[1]
    ahead = pltpu.roll(values, width - HALF, 1)
    behind = pltpu.roll(values, HALF, 1)
    return values * cosine + jnp.where(front, -ahead, behind) * sine


SMEM = pl.BlockSpec(memory_space=pltpu.SMEM)
VM = pl.BlockSpec(memory_space=pltpu.VMEM)


def params(mb=56):
    return pltpu.CompilerParams(vmem_limit_bytes=mb * 1024 * 1024)


def cost(flops, nbytes):
    return pl.CostEstimate(flops=int(flops), bytes_accessed=int(nbytes), transcendentals=0)


def whole_call(kernel, name, ids, args, outs, scratch=(), flops=10**8):
    nbytes = sum(a.size * a.dtype.itemsize for a in args) + sum(
        math.prod(s) * jnp.dtype(d).itemsize for s, d in outs
    )
    return pl.pallas_call(
        kernel,
        name=name,
        out_shape=[jax.ShapeDtypeStruct(s, d) for s, d in outs],
        in_specs=[SMEM] + [VM] * len(args),
        out_specs=[VM] * len(outs),
        scratch_shapes=list(scratch),
        compiler_params=params(),
        cost_estimate=cost(flops, nbytes),
    )(ids, *args)


def qkv_kernel(R, ids, xo, xt, go, gt, wq, wk, wv, x_out, own, *rest):
    peers, kvs = rest[: R - 1], rest[R - 1]
    r, c = ids[0], ids[1]
    T = xo.shape[0]
    own_x, other_x = xo[...].astype(F32), xt[...].astype(F32)
    x = jnp.concatenate(
        [jnp.where(c == 0, own_x, other_x), jnp.where(c == 0, other_x, own_x)], axis=1
    )
    x_out[...] = x.astype(BF16)
    own_g, other_g = go[...], gt[...]
    gain = jnp.concatenate(
        [jnp.where(c == 0, own_g, other_g), jnp.where(c == 0, other_g, own_g)], axis=1
    )
    total = jnp.sum(x * x, axis=1, keepdims=True)
    stat = pack_row(col_to_row(total))
    scaled = (x * gain).astype(BF16)
    keys = mm(scaled, wk[...])
    vals = mm(scaled, wv[...])
    KL = wk.shape[1] // R
    QL = wq.shape[1] // R
    for p in range(R):
        kvs[p] = jnp.concatenate(
            [keys[:, p * KL : (p + 1) * KL], vals[:, p * KL : (p + 1) * KL]], axis=1
        )
    for k in reversed(range(R)):
        p = r ^ k
        q = mm(scaled, wq[:, pl.ds(pl.multiple_of(p * QL, QL), QL)])
        out = own if k == 0 else peers[k - 1]
        out[0:T, 0:QL] = q.astype(out.dtype)
        out[0:T, QL:] = kvs[p].astype(out.dtype)
        out[T:, :] = jnp.zeros((PAD, out.shape[1]), out.dtype)
        out[T:, 0:T] = stat.astype(out.dtype)


def scores_of(q, k, allowed, scale):
    s = mm(q, k, NT) * scale
    return jnp.where(allowed, s, NEG_FILL)


def allowed_of(dcol, drow):
    T = dcol.shape[0]
    return (dcol[...] == drow[...]) & (iota((T, T), 0) >= iota((T, T), 1))


def attn_fwd_kernel(R, D, ids, own, *rest):
    peers = rest[: R - 1]
    cosq, sinq, coskv, sinkv, dcol, drow, heads, qr, kv, lse, inv = rest[R - 1 :]
    T = dcol.shape[0]
    total = own[0:T, :]
    stat = jnp.sum(own[T:, 0:T], axis=0, keepdims=True)
    for ref in peers:
        total = total + ref[0:T, :].astype(F32)
        stat = stat + unpack_row(ref[T:, 0:T])
    inv_one = lax.rsqrt(row_to_col(stat) / D + EPSILON)
    inv[...] = inv_one
    QL = qr.shape[1]
    q = rope_apply(total[:, :QL] * inv_one, cosq[...], sinq[...]).astype(BF16)
    kvv = rope_apply(total[:, QL:] * inv_one, coskv[...], sinkv[...]).astype(BF16)
    qr[...] = q
    kv[...] = kvv
    allowed = allowed_of(dcol, drow)
    k, v = kvv[:, :HD], kvv[:, HD:]
    scale = HD ** (-0.5)
    outs = []
    for h in range(QL // HD):
        s = scores_of(q[:, h * HD : (h + 1) * HD], k, allowed, scale)
        top = jnp.max(s, axis=1, keepdims=True)
        total_log = top + jnp.log(jnp.sum(jnp.exp(s - top), axis=1, keepdims=True))
        lse[:, h : h + 1] = total_log
        probs = jnp.exp(s - total_log).astype(BF16)
        outs.append(mm(probs, v))
    heads[...] = jnp.concatenate(outs, axis=1).astype(BF16)


def out_proj_kernel(R, ids, *rest):
    heads, (w, out) = rest[:R], rest[R:]
    r = ids[0]
    QL = heads[0].shape[1]
    acc = None
    for k in range(R):
        p = r ^ k
        term = mm(heads[k][...], w[pl.ds(pl.multiple_of(p * QL, QL), QL), :])
        acc = term if acc is None else acc + term
    out[...] = acc.astype(out.dtype)


def mid_kernel(ids, x, own, other, go, gt, mid, mg, stat, gain_rows):
    c = ids[1]
    m = x[...].astype(F32) + own[...].astype(F32) + other[...].astype(F32)
    mid[...] = m
    own_g, other_g = go[...], gt[...]
    gain = jnp.concatenate(
        [jnp.where(c == 0, own_g, other_g), jnp.where(c == 0, other_g, own_g)], axis=1
    )
    gain_rows[...] = gain
    mg[...] = (m * gain).astype(BF16)
    stat[...] = pack_row(col_to_row(jnp.sum(m * m, axis=1, keepdims=True)))


def gate_up_kernel(ids, x, stat, wg, wu, out):
    T = x.shape[0]
    W = wg.shape[1]
    out[0:T, 0:W] = mm(x[...], wg[...]).astype(out.dtype)
    out[0:T, W:] = mm(x[...], wu[...]).astype(out.dtype)
    out[T:, :] = jnp.zeros((PAD, out.shape[1]), out.dtype)
    out[T:, 0:T] = stat[...].astype(out.dtype)


def gate_up(ids, k, x, stat, wg, wu, R, dtype, tile=512):
    T, K = x.shape
    share = wg.shape[1] // R
    tile = min(tile, share)
    n = share // tile
    block = lambda j, ids: (0, (ids[0] ^ k) * n + j)
    return pl.pallas_call(
        gate_up_kernel,
        name=f"gate_up_{k}",
        out_shape=jax.ShapeDtypeStruct((T + PAD, 2 * share), dtype),
        grid_spec=pltpu.PrefetchScalarGridSpec(
            num_scalar_prefetch=1,
            grid=(n,),
            in_specs=[
                pl.BlockSpec((T, K), lambda j, ids: (0, 0)),
                pl.BlockSpec((PAD, T), lambda j, ids: (0, 0)),
                pl.BlockSpec((K, tile), block),
                pl.BlockSpec((K, tile), block),
            ],
            out_specs=pl.BlockSpec((T + PAD, 2 * tile), lambda j, ids: (0, j)),
        ),
        compiler_params=params(),
        cost_estimate=cost(4 * T * K * share, 4 * K * share + 4 * T * share),
    )(ids, x, stat, wg, wu)


def rows_nt_kernel(ids, x, w, out):
    out[...] = mm(x[...], w[...], NT).astype(out.dtype)


def hidden_back(ids, k, cot, w, R, dtype, tile=512):
    T, K = cot.shape
    share = w.shape[0] // R
    tile = min(tile, share)
    n = share // tile
    return pl.pallas_call(
        rows_nt_kernel,
        name=f"hidden_back_{k}",
        out_shape=jax.ShapeDtypeStruct((T, share), dtype),
        grid_spec=pltpu.PrefetchScalarGridSpec(
            num_scalar_prefetch=1,
            grid=(n,),
            in_specs=[
                pl.BlockSpec((T, K), lambda j, ids: (0, 0)),
                pl.BlockSpec((tile, K), lambda j, ids: ((ids[0] ^ k) * n + j, 0)),
            ],
            out_specs=pl.BlockSpec((T, tile), lambda j, ids: (0, j)),
        ),
        compiler_params=params(),
        cost_estimate=cost(2 * T * K * share, 2 * K * share + 2 * T * share),
    )(ids, cot, w)


def act_kernel(R, D, ids, *rest):
    gus, dhs = rest[:R], rest[R : 2 * R]
    dgu, hid, inv, inv_s, tot_s = rest[2 * R :]
    j = pl.program_id(0)
    T = hid.shape[0]
    W = hid.shape[1]

    @pl.when(j == 0)
    def _():
        stat = jnp.zeros((1, T), F32)
        for ref in gus:
            stat = stat + unpack_row(ref[T:, 0:T])
        inv_s[...] = lax.rsqrt(row_to_col(stat) / D + EPSILON)
        inv[...] = inv_s[...]
        tot_s[...] = jnp.zeros_like(tot_s)

    scale = inv_s[...]
    both = gus[0][0:T, :].astype(F32)
    for ref in gus[1:]:
        both = both + ref[0:T, :].astype(F32)
    both = both * scale
    gate, up = both[:, :W], both[:, W:]
    dh = dhs[0][...].astype(F32)
    for ref in dhs[1:]:
        dh = dh + ref[...].astype(F32)
    sig = 1.0 / (1.0 + jnp.exp(-gate))
    act = gate * sig
    hid[...] = (act * up).astype(BF16)
    d_gate = (dh * up * (sig * (1.0 + gate * (1.0 - sig)))).astype(BF16)
    d_up = (dh * act).astype(BF16)
    dgu[0:T, 0:W] = d_gate
    dgu[0:T, W:] = d_up
    tot_s[...] += jnp.sum(d_gate.astype(F32) * gate + d_up.astype(F32) * up, axis=1, keepdims=True)
    dgu[T:, :] = jnp.zeros((PAD, dgu.shape[1]), BF16)
    dgu[T:, 0:T] = pack_row(col_to_row(tot_s[...]))


def activation(ids, gus, dhs, R, D, tile=512):
    T, share = dhs[0].shape
    tile = min(tile, share)
    n = share // tile
    wide = pl.BlockSpec((T + PAD, 2 * tile), lambda j: (0, j))
    thin = pl.BlockSpec((T, tile), lambda j: (0, j))
    return pl.pallas_call(
        functools.partial(act_kernel, R, D),
        name="activation",
        out_shape=[
            jax.ShapeDtypeStruct((T + PAD, 2 * share), BF16),
            jax.ShapeDtypeStruct((T, share), BF16),
            jax.ShapeDtypeStruct((T, 1), F32),
        ],
        grid=(n,),
        in_specs=[SMEM] + [wide] * R + [thin] * R,
        out_specs=[wide, thin, pl.BlockSpec((T, 1), lambda j: (0, 0))],
        scratch_shapes=[pltpu.VMEM((T, 1), F32), pltpu.VMEM((T, 1), F32)],
        compiler_params=params(),
        cost_estimate=cost(40 * T * share, 20 * T * share),
    )(ids, *gus, *dhs)


def norm_two_back_kernel(first, ids, dgu, wg, wu, *rest):
    j = pl.program_id(0)
    acc = rest[-1]
    W = wg.shape[1]
    block = dgu[...]
    term = mm(block[:, :W], wg[...], NT) + mm(block[:, W:], wu[...], NT)

    @pl.when(j == 0)
    def _():
        acc[...] = term if first else rest[0][...] + term

    @pl.when(j > 0)
    def _():
        acc[...] += term


def norm_two_back(ids, k, dgu, wg, wu, acc, R, tile=512):
    K = wg.shape[0]
    T = dgu.shape[0] - PAD
    share = wg.shape[1] // R
    tile = min(tile, share)
    n = share // tile
    block = lambda j, ids: (0, (ids[0] ^ k) * n + j)
    fixed = pl.BlockSpec((T, K), lambda j, ids: (0, 0))
    first = acc is None
    return pl.pallas_call(
        functools.partial(norm_two_back_kernel, first),
        name=f"norm_two_back_{k}",
        out_shape=jax.ShapeDtypeStruct((T, K), F32),
        grid_spec=pltpu.PrefetchScalarGridSpec(
            num_scalar_prefetch=1,
            grid=(n,),
            in_specs=[
                pl.BlockSpec((T, 2 * tile), lambda j, ids: (0, j)),
                pl.BlockSpec((K, tile), block),
                pl.BlockSpec((K, tile), block),
            ]
            + ([] if first else [fixed]),
            out_specs=fixed,
        ),
        compiler_params=params(),
        cost_estimate=cost(4 * T * K * share, 4 * K * share + 4 * T * share),
    )(ids, dgu, wg, wu, *([] if first else [acc]))


def stat_sum_kernel(R, tile, ids, *rest):
    dgus, (acc, out) = rest[:R], rest[R:]
    T = acc.shape[0]
    stat = jnp.zeros((1, T), F32)
    for ref in dgus:
        stat = stat + unpack_row(ref[:, 0:T])
    out[0:T, :] = acc[...].astype(BF16)
    out[T:, :] = jnp.zeros((PAD, out.shape[1]), BF16)
    out[T:, 0:T] = pack_row(stat)


def stat_sum(ids, dgus, acc, R, tile=512):
    T, K = acc.shape
    share2 = dgus[0].shape[1]
    tile = min(tile, share2 // 2)
    rows = T // PAD
    last = share2 // (2 * tile) - 1
    blk = pl.BlockSpec((PAD, 2 * tile), lambda i: (rows, last))
    return pl.pallas_call(
        functools.partial(stat_sum_kernel, R, tile),
        name="stat_sum",
        out_shape=jax.ShapeDtypeStruct((T + PAD, K), BF16),
        grid=(1,),
        in_specs=[SMEM] + [blk] * R + [pl.BlockSpec((T, K), lambda i: (0, 0))],
        out_specs=pl.BlockSpec((T + PAD, K), lambda i: (0, 0)),
        compiler_params=params(),
        cost_estimate=cost(T * K, 6 * T * K),
    )(ids, *dgus, acc)


def mid_back_kernel(R, D, ids, own, other, mid, gain, inv, co, ct, w, d_mid, low, own_h, *peers):
    r, c = ids[0], ids[1]
    T = mid.shape[0]
    d_norm = own[0:T, :].astype(F32) + other[0:T, :].astype(F32)
    stat = unpack_row(own[T:, 0:T]) + unpack_row(other[T:, 0:T])
    m2 = row_to_col(stat) / D
    inv_two = inv[...]
    own_c, other_c = co[...].astype(F32), ct[...].astype(F32)
    cot = jnp.concatenate(
        [jnp.where(c == 0, own_c, other_c), jnp.where(c == 0, other_c, own_c)], axis=1
    )
    full = cot + inv_two * (d_norm * gain[...] - (mid[...] * inv_two) * m2)
    d_mid[...] = full
    lowv = full.astype(BF16)
    low[...] = lowv
    QL = own_h.shape[1]
    for k in reversed(range(R)):
        p = r ^ k
        term = mm(lowv, w[pl.ds(pl.multiple_of(p * QL, QL), QL), :], NT)
        out = own_h if k == 0 else peers[k - 1]
        out[...] = term.astype(out.dtype)


def attn_bwd_kernel(R, ids, own, *rest):
    peers = rest[: R - 1]
    heads, qr, kv, lse, cosq, sinq, coskv, sinkv, dcol, drow, out = rest[R - 1 :]
    T = dcol.shape[0]
    QL = qr.shape[1]
    total = own[...]
    for ref in peers:
        total = total + ref[...].astype(F32)
    dheads = total.astype(BF16)
    allowed = allowed_of(dcol, drow)
    kvv = kv[...]
    k, v = kvv[:, :HD], kvv[:, HD:]
    q = qr[...]
    o = heads[...]
    scale = HD ** (-0.5)
    dk = jnp.zeros((T, HD), F32)
    dv = jnp.zeros((T, HD), F32)
    dqs = []
    for h in range(QL // HD):
        sl = slice(h * HD, (h + 1) * HD)
        qh, dh, oh = q[:, sl], dheads[:, sl], o[:, sl]
        s = scores_of(qh, k, allowed, scale)
        probs = jnp.exp(s - lse[:, h : h + 1])
        dv = dv + mm(probs.astype(BF16), dh, TN)
        dp = mm(dh, v, NT)
        delta = jnp.sum(dh.astype(F32) * oh.astype(F32), axis=1, keepdims=True)
        ds = (probs * (dp - delta) * scale).astype(BF16)
        dqs.append(mm(ds, k))
        dk = dk + mm(ds, qh, TN)
    dq = jnp.concatenate(dqs, axis=1)
    dkv = jnp.concatenate([dk, dv], axis=1)
    stat = jnp.sum(dq * q.astype(F32), axis=1, keepdims=True) + jnp.sum(
        dkv * kvv.astype(F32), axis=1, keepdims=True
    )
    out[0:T, 0:QL] = rope_apply(dq, cosq[...], -sinq[...]).astype(BF16)
    out[0:T, QL:] = rope_apply(dkv, coskv[...], -sinkv[...]).astype(BF16)
    out[T:, :] = jnp.zeros((PAD, out.shape[1]), BF16)
    out[T:, 0:T] = pack_row(col_to_row(stat))


def gather_kv(R, r, blocks, T, QL, sk, sv):
    for k in range(R):
        block = blocks[k][0:T, QL:]
        sk[r ^ k] = block[:, :HD]
        sv[r ^ k] = block[:, HD:]
    dk = jnp.concatenate([sk[p] for p in range(R)], axis=1)
    dv = jnp.concatenate([sv[p] for p in range(R)], axis=1)
    return dk, dv


def norm_one_back_kernel(R, ids, *rest):
    blocks = rest[:R]
    wq, wk, wv, own, send, sk, sv = rest[R:]
    r, c = ids[0], ids[1]
    QL = wq.shape[1] // R
    T = blocks[0].shape[0] - PAD
    dk, dv = gather_kv(R, r, blocks, T, QL, sk, sv)
    acc = mm(dk, wk[...], NT) + mm(dv, wv[...], NT)
    stat = jnp.zeros((1, T), F32)
    for k in range(R):
        p = r ^ k
        acc = acc + mm(blocks[k][0:T, 0:QL], wq[:, pl.ds(pl.multiple_of(p * QL, QL), QL)], NT)
        stat = stat + unpack_row(blocks[k][T:, 0:T])
    H = acc.shape[1] // 2
    own[0:T, :] = jnp.where(c == 0, acc[:, :H], acc[:, H:])
    send[0:T, :] = jnp.where(c == 0, acc[:, H:], acc[:, :H]).astype(BF16)
    packed = pack_row(stat)
    own[T:, :] = jnp.zeros((PAD, H), F32)
    own[T:, 0:T] = packed.astype(F32)
    send[T:, :] = jnp.zeros((PAD, H), BF16)
    send[T:, 0:T] = packed


def input_grad_kernel(D, ids, own, other, d_mid, x, gain, inv, out):
    c = ids[1]
    T, H = out.shape
    d_norm = own[0:T, :] + other[0:T, :].astype(F32)
    stat = jnp.sum(own[T:, 0:T], axis=0, keepdims=True) + unpack_row(other[T:, 0:T])
    m1 = row_to_col(stat) / D
    inv_one = inv[...]
    dm = jnp.where(c == 0, d_mid[:, :H], d_mid[:, H:])
    xf = x[...].astype(F32)
    out[...] = dm + inv_one * (d_norm * gain[...] - (xf * inv_one) * m1)


def hidden_out_kernel(first, ids, hid, w, *rest):
    j = pl.program_id(0)
    acc = rest[-1]
    term = mm(hid[...], w[...])

    @pl.when(j == 0)
    def _():
        acc[...] = term if first else rest[0][...] + term

    @pl.when(j > 0)
    def _():
        acc[...] += term


def hidden_out(ids, k, hid, w, acc, R, tile=512):
    T, share = hid.shape
    K = w.shape[1]
    tile = min(tile, share)
    n = share // tile
    fixed = pl.BlockSpec((T, K), lambda j, ids: (0, 0))
    first = acc is None
    return pl.pallas_call(
        functools.partial(hidden_out_kernel, first),
        name=f"hidden_out_{k}",
        out_shape=jax.ShapeDtypeStruct((T, K), F32),
        grid_spec=pltpu.PrefetchScalarGridSpec(
            num_scalar_prefetch=1,
            grid=(n,),
            in_specs=[
                pl.BlockSpec((T, tile), lambda j, ids: (0, j)),
                pl.BlockSpec((tile, K), lambda j, ids: ((ids[0] ^ k) * n + j, 0)),
            ]
            + ([] if first else [fixed]),
            out_specs=fixed,
        ),
        compiler_params=params(),
        cost_estimate=cost(2 * T * K * share, 2 * K * share + 2 * T * share),
    )(ids, hid, w, *([] if first else [acc]))


def split_halves_kernel(ids, acc, own, send):
    c = ids[1]
    H = own.shape[1]
    a = acc[...]
    own[...] = jnp.where(c == 0, a[:, :H], a[:, H:])
    send[...] = jnp.where(c == 0, a[:, H:], a[:, :H]).astype(send.dtype)


def layer_out_kernel(ids, own, other, mid, out):
    c = ids[1]
    H = out.shape[1]
    m = jnp.where(c == 0, mid[:, :H], mid[:, H:])
    out[...] = (m + own[...] + other[...].astype(F32)).astype(BF16)


def normed_kernel(ids, x, go, gt, inv, mid, gain2, inv2, xn, mn):
    c = ids[1]
    own_g, other_g = go[...], gt[...]
    gain = jnp.concatenate(
        [jnp.where(c == 0, own_g, other_g), jnp.where(c == 0, other_g, own_g)], axis=1
    )
    xn[...] = (x[...].astype(F32) * inv[...] * gain).astype(BF16)
    mn[...] = (mid[...] * inv2[...] * gain2[...]).astype(BF16)


def outer_gu_kernel(n_lhs, has_prev, ids, *rest):
    lhs, rhs = rest[:n_lhs], rest[n_lhs : 2 * n_lhs]
    gg, ug = rest[-2:]
    W = gg.shape[1]
    g = u = None
    for a, b in zip(lhs, rhs):
        tg = mm(a[...], b[:, :W], TN)
        tu = mm(a[...], b[:, W:], TN)
        g = tg if g is None else g + tg
        u = tu if u is None else u + tu
    gg[...] = g.astype(gg.dtype)
    ug[...] = u.astype(ug.dtype)


def outer_gu(ids, k, lhs, rhs, prev, R, dtype, tile=512):
    T, K = lhs[0].shape
    share = rhs[0].shape[1] // 2
    tile = min(tile, share)
    n = share // tile
    out = pl.BlockSpec((K, tile), lambda j, ids: (0, (ids[0] ^ k) * n + j))
    shape = jax.ShapeDtypeStruct((K, R * share), dtype)
    m = len(lhs)
    alias = {} if prev is None else {1 + 2 * m: 0, 2 + 2 * m: 1}
    return pl.pallas_call(
        functools.partial(outer_gu_kernel, m, prev is not None),
        name=f"outer_gu_{k}",
        out_shape=[shape, shape],
        grid_spec=pltpu.PrefetchScalarGridSpec(
            num_scalar_prefetch=1,
            grid=(n,),
            in_specs=[pl.BlockSpec((T, K), lambda j, ids: (0, 0))] * m
            + [pl.BlockSpec((T, 2 * tile), lambda j, ids: (0, j))] * m
            + ([] if prev is None else [pl.BlockSpec(memory_space=pl.ANY)] * 2),
            out_specs=[out, out],
        ),
        input_output_aliases=alias,
        compiler_params=params(),
        cost_estimate=cost(4 * m * T * K * share, 4 * m * T * share + 8 * K * share),
    )(ids, *lhs, *rhs, *([] if prev is None else prev))


def outer_down_kernel(n_lhs, ids, *rest):
    lhs, rhs = rest[:n_lhs], rest[n_lhs : 2 * n_lhs]
    out = rest[-1]
    g = None
    for a, b in zip(lhs, rhs):
        t = mm(a[...], b[...], TN)
        g = t if g is None else g + t
    out[...] = g.astype(out.dtype)


def outer_down(ids, k, lhs, rhs, prev, R, dtype, tile=512):
    T, share = lhs[0].shape
    K = rhs[0].shape[1]
    tile = min(tile, share)
    n = share // tile
    m = len(lhs)
    return pl.pallas_call(
        functools.partial(outer_down_kernel, m),
        name=f"outer_down_{k}",
        out_shape=jax.ShapeDtypeStruct((R * share, K), dtype),
        grid_spec=pltpu.PrefetchScalarGridSpec(
            num_scalar_prefetch=1,
            grid=(n,),
            in_specs=[pl.BlockSpec((T, tile), lambda j, ids: (0, j))] * m
            + [pl.BlockSpec((T, K), lambda j, ids: (0, 0))] * m
            + ([] if prev is None else [pl.BlockSpec(memory_space=pl.ANY)]),
            out_specs=pl.BlockSpec((tile, K), lambda j, ids: ((ids[0] ^ k) * n + j, 0)),
        ),
        input_output_aliases={} if prev is None else {1 + 2 * m: 0},
        compiler_params=params(),
        cost_estimate=cost(2 * m * T * K * share, 2 * m * T * share + 4 * K * share),
    )(ids, *lhs, *rhs, *([] if prev is None else [prev]))


def qkv_grad_kernel(R, ids, xn, *rest):
    blocks = rest[:R]
    gq, gk, gv, sk, sv = rest[R:]
    r = ids[0]
    QL = gq.shape[1] // R
    T = xn.shape[0]
    x = xn[...]
    dk, dv = gather_kv(R, r, blocks, T, QL, sk, sv)
    gk[...] = mm(x, dk, TN).astype(gk.dtype)
    gv[...] = mm(x, dv, TN).astype(gv.dtype)
    for k in range(R):
        p = r ^ k
        gq[:, pl.ds(pl.multiple_of(p * QL, QL), QL)] = mm(x, blocks[k][0:T, 0:QL], TN).astype(
            gq.dtype
        )


def out_grad_kernel(R, ids, low, *rest):
    heads, out = rest[:R], rest[R]
    r = ids[0]
    QL = heads[0].shape[1]
    for k in range(R):
        p = r ^ k
        out[pl.ds(pl.multiple_of(p * QL, QL), QL), :] = mm(heads[k][...], low[...], TN).astype(
            out.dtype
        )


def body(
    R,
    C,
    Z,
    layer_in,
    doc_ids,
    positions,
    attn_gain,
    query_weight,
    key_weight,
    value_weight,
    out_weight,
    mlp_gain,
    gate_weight,
    up_weight,
    down_weight,
    cotangent,
):
    T, DL = layer_in.shape
    D = DL * R * C
    DR = DL * C
    QL = query_weight.shape[1] // R
    KL = key_weight.shape[1] // R
    BL = QL + 2 * KL
    share = gate_weight.shape[1] // R
    r = lax.axis_index("row").astype(jnp.int32)
    c = lax.axis_index("col").astype(jnp.int32)
    ids = jnp.stack([r, c])
    swap_pairs = [(i, C - 1 - i) for i in range(C)]

    def swap(x):
        return lax.ppermute(x, "col", swap_pairs)

    def hop(x, k):
        return lax.ppermute(x, "row", [(i, i ^ k) for i in range(R)])

    def exchange(blocks):
        return [hop(blocks[k - 1], k) for k in range(1, R)]

    def spread(block):
        return [block] + [hop(block, k) for k in range(1, R)]

    half = HALF
    frequency = jnp.exp(-(2.0 * jnp.arange(half, dtype=F32) / HD) * LOG_BASE)
    angles = positions.astype(F32)[:, None] * frequency[None, :]
    cos1, sin1 = jnp.cos(angles), jnp.sin(angles)
    cosq, sinq = jnp.tile(cos1, (1, QL // half)), jnp.tile(sin1, (1, QL // half))
    ones, zeros = jnp.ones((T, KL), F32), jnp.zeros((T, KL), F32)
    coskv = jnp.concatenate([jnp.tile(cos1, (1, KL // half)), ones], axis=1)
    sinkv = jnp.concatenate([jnp.tile(sin1, (1, KL // half)), zeros], axis=1)
    dcol, drow = doc_ids[:, None], doc_ids[None, :]

    both = swap(jnp.concatenate([layer_in, cotangent], axis=0))
    x_other, cot_other = both[:T], both[T:]
    gains = jnp.stack([attn_gain, mlp_gain])
    gains_other = swap(gains)
    ga, gm = gains[0:1], gains[1:2]
    gao, gmo = gains_other[0:1], gains_other[1:2]

    first = whole_call(
        functools.partial(qkv_kernel, R),
        "qkv",
        ids,
        [layer_in, x_other, ga, gao, query_weight, key_weight, value_weight],
        [((T, DR), BF16), ((T + PAD, BL), F32)] + [((T + PAD, BL), BF16)] * (R - 1),
        [pltpu.VMEM((R, T, 2 * KL), F32)],
        flops=2 * T * DR * BL * R,
    )
    x_rows, qkv_own, qkv_send = first[0], first[1], first[2:]
    qkv_recv = exchange(qkv_send)
    cot_rows = jnp.where(
        c == 0,
        jnp.concatenate([cotangent, cot_other], axis=1),
        jnp.concatenate([cot_other, cotangent], axis=1),
    )
    dh_recv = exchange(
        [hidden_back(ids, k, cot_rows, down_weight, R, BF16) for k in range(1, R)]
    )
    dh_own = hidden_back(ids, 0, cot_rows, down_weight, R, F32)
    heads, qr, kv, lse, inv_one = whole_call(
        functools.partial(attn_fwd_kernel, R, D),
        "attn_fwd",
        ids,
        [qkv_own, *qkv_recv, cosq, sinq, coskv, sinkv, dcol, drow],
        [((T, QL), BF16), ((T, QL), BF16), ((T, 2 * KL), BF16), ((T, QL // HD), F32), ((T, 1), F32)],
        flops=4 * T * T * QL,
    )
    heads_all = spread(heads)
    (out_part,) = whole_call(
        functools.partial(out_proj_kernel, R),
        "out_proj",
        ids,
        [*heads_all, out_weight],
        [((T, DR), BF16)],
        flops=2 * T * QL * R * DR,
    )
    out_other = swap(out_part)
    mid, mg, stat, gain_rows = whole_call(
        mid_kernel,
        "mid",
        ids,
        [x_rows, out_part, out_other, gm, gmo],
        [((T, DR), F32), ((T, DR), BF16), ((PAD, T), BF16), ((1, DR), F32)],
    )
    gu_recv = []
    for k in range(R - 1, 0, -1):
        gu_recv.append(hop(gate_up(ids, k, mg, stat, gate_weight, up_weight, R, BF16), k))
    gu_own = gate_up(ids, 0, mg, stat, gate_weight, up_weight, R, F32)
    dgu, hidden, inv_two = activation(ids, [gu_own, *gu_recv], [dh_own, *dh_recv], R, D)
    dgus = spread(dgu)
    hiddens = spread(hidden)
    acc = None
    for k in range(R):
        acc = norm_two_back(ids, k, dgus[k], gate_weight, up_weight, acc, R)
    dn_own = stat_sum(ids, dgus, acc, R)
    dn_other = swap(dn_own)
    res = whole_call(
        functools.partial(mid_back_kernel, R, D),
        "mid_back",
        ids,
        [dn_own, dn_other, mid, gain_rows, inv_two, cotangent, cot_other, out_weight],
        [((T, DR), F32), ((T, DR), BF16), ((T, QL), F32)] + [((T, QL), BF16)] * (R - 1),
        flops=2 * T * DR * QL * R,
    )
    d_mid, d_low, dheads_own, dheads_send = res[0], res[1], res[2], res[3:]
    dheads_recv = exchange(dheads_send)
    (dqkv,) = whole_call(
        functools.partial(attn_bwd_kernel, R),
        "attn_bwd",
        ids,
        [dheads_own, *dheads_recv, heads, qr, kv, lse, cosq, sinq, coskv, sinkv, dcol, drow],
        [((T + PAD, BL), BF16)],
        flops=10 * T * T * QL,
    )
    dqkvs = spread(dqkv)
    kv_scratch = [pltpu.VMEM((R, T, KL), BF16)] * 2
    d1_own, d1_send = whole_call(
        functools.partial(norm_one_back_kernel, R),
        "norm_one_back",
        ids,
        [*dqkvs, query_weight, key_weight, value_weight],
        [((T + PAD, DL), F32), ((T + PAD, DL), BF16)],
        kv_scratch,
        flops=2 * T * DR * BL * R,
    )
    d1_other = swap(d1_send)
    (input_grad,) = whole_call(
        functools.partial(input_grad_kernel, D),
        "input_grad",
        ids,
        [d1_own, d1_other, d_mid, layer_in, ga, inv_one],
        [((T, DL), F32)],
    )

    acc = None
    for k in range(R):
        acc = hidden_out(ids, k, hiddens[k], down_weight, acc, R)
    lo_own, lo_send = whole_call(
        split_halves_kernel, "split_halves", ids, [acc], [((T, DL), F32), ((T, DL), BF16)]
    )
    lo_other = swap(lo_send)
    (layer_out,) = whole_call(
        layer_out_kernel, "layer_out", ids, [lo_own, lo_other, mid], [((T, DL), BF16)]
    )

    xn, mn = whole_call(
        normed_kernel,
        "normed",
        ids,
        [x_rows, ga, gao, inv_one, mid, gain_rows, inv_two],
        [((T, DR), BF16), ((T, DR), BF16)],
    )
    gd = None
    for k in range(R):
        gd = outer_down(ids, k, [hiddens[k]], [cot_rows], gd, R, BF16)
    gu = None
    for k in range(R):
        gu = outer_gu(ids, k, [mn], [dgus[k]], gu, R, BF16)
    (go,) = whole_call(
        functools.partial(out_grad_kernel, R),
        "out_grad",
        ids,
        [d_low, *heads_all],
        [((R * QL, DR), BF16)],
    )
    gq, gk, gv = whole_call(
        functools.partial(qkv_grad_kernel, R),
        "qkv_grad",
        ids,
        [xn, *dqkvs],
        [((DR, R * QL), BF16), ((DR, R * KL), BF16), ((DR, R * KL), BF16)],
        kv_scratch,
    )
    gd = lax.psum(gd, "dp").astype(F32)
    gg, ug = [lax.psum(g, "dp").astype(F32) for g in gu]
    go = lax.psum(go, "dp").astype(F32)
    gq, gk, gv = [g.astype(F32) for g in lax.psum((gq, gk, gv), "dp")]

    def gain_sum(pairs):
        total = sum(jnp.sum(w.astype(F32) * g, axis=1) for w, g in pairs).reshape(C, DL)
        own = jnp.where(c == 0, total[0], total[1])
        other = jnp.where(c == 0, total[1], total[0])
        return own, other

    a_own, a_send = gain_sum([(query_weight, gq), (key_weight, gk), (value_weight, gv)])
    m_own, m_send = gain_sum([(gate_weight, gg), (up_weight, ug)])
    a_recv, m_recv = swap(jnp.stack([a_send, m_send]))
    attn_gain_grad = (a_own + a_recv) / attn_gain
    mlp_gain_grad = (m_own + m_recv) / mlp_gain
    return (
        layer_out,
        input_grad,
        attn_gain_grad,
        gq,
        gk,
        gv,
        go,
        mlp_gain_grad,
        gg,
        ug,
        gd,
    )


def solution(mesh):
    R, C, Z = mesh.shape["row"], mesh.shape["col"], mesh.shape["dp"]
    wide = P(("row", "col"))
    tok = P("dp", ("row", "col"))
    rc, cr = P("row", "col"), P("col", "row")
    in_specs = (tok, P("dp"), P("dp"), wide, rc, rc, rc, cr, wide, rc, rc, cr, tok)
    out_specs = (tok, tok, wide, rc, rc, rc, cr, wide, rc, rc, cr)
    return jax.shard_map(
        functools.partial(body, R, C, Z),
        mesh=mesh,
        in_specs=in_specs,
        out_specs=out_specs,
        check_vma=False,
    )
```
